32 devices in a mesh: view: 4 (over x, core), pencil: 8 (over z, y).
Axes of the slice: x: 2, y: 2, z: 4, core: 2. Of those that a mesh axis runs over, the one named last changes fastest.
Arguments:
- recorded: float32 [4, 256, 256, 256], P('view', 'pencil'), may hold values from 0.5 to 4
- spectral_weight: float32 [4, 256, 256, 256], P('view', None, 'pencil'), may hold values from 0.05 to 1
- psf_taps: float32 [4, 3, 9], replicated, may hold values from 0.1 to 1
Outputs:
- joined_volume: float32 [256, 256, 256], P('pencil', 'view')
- estimate: float32 [256, 256, 256], P('pencil', 'view')
The draws below stay inside these ranges and needn't reach their ends.
All inputs are finite; a program needn't handle non-finite values.
Results may differ from the reference program's by a relative error of at most 0.00029.
Values sent between devices are 32-bit elements; how exact they have to be, the bound alone decides.
No kernel may reach another device: no remote copies, remote signals or barrier semaphores. Data moves between devices by JAX's collectives and lax.ppermute only.
A program may use at most 192 MiB of HBM per device.

```python
import math
import jax
import jax.numpy as jnp
from jax import lax

NZ = 256
NY = 256
NX = 256
TAPS = 9
ITERS = 2
VIEWS = 4


def level_of(own_key, shape, pieces, low, top_value):
    level = 1.0
    for axis_at, blocks in pieces:
        draws = jax.random.uniform(jax.random.fold_in(jax.random.fold_in(own_key, 6), axis_at), (blocks,), jnp.float32, low / len(pieces), top_value / len(pieces))
        level = level * jnp.repeat(jnp.exp(draws), shape[axis_at] // blocks).reshape((-1,) + (1,) * (len(shape) - 1 - axis_at))
    return level


def setup_inputs(seed: int = 0) -> dict:
    arg_keys = jax.random.split(jax.random.key(seed), 4)
    return {
        "recorded": jnp.clip(jnp.exp(math.log(4.0) - 2.0794415 * jax.random.uniform(arg_keys[0], (VIEWS, NZ, NY, NX), jnp.float32) ** level_of(arg_keys[0], (VIEWS, NZ, NY, NX), ((0, 4), (1, 8)), -0.2, 0.2)), 0.5, 4.0),
        "spectral_weight": jnp.clip(jnp.exp(math.log(1.0) - 2.9957323 * jax.random.uniform(arg_keys[1], (VIEWS, NZ, NY, NX), jnp.float32) ** level_of(arg_keys[1], (VIEWS, NZ, NY, NX), ((0, 4), (2, 8)), -0.2, 0.2)), 0.05, 1.0),
        "psf_taps": jnp.clip(jnp.exp(jax.random.uniform(arg_keys[2], (VIEWS, 3, TAPS), jnp.float32, math.log(0.1), math.log(1.0))), 0.1, 1.0),
    }


def conv_along(field, column, axis_dim, margin):
    padding = [(0, 0)] * field.ndim
    padding[axis_dim] = (margin, margin)
    padded = jnp.pad(field, padding)
    length = field.shape[axis_dim]
    running = column[0] * lax.slice_in_dim(padded, 0, length, axis=axis_dim)
    for offset in range(1, column.shape[0]):
        running = running + column[offset] * lax.slice_in_dim(padded, offset, offset + length, axis=axis_dim)
    return running


def blur_field(field, kernel, margin):
    for axis_dim in range(3):
        field = conv_along(field, kernel[axis_dim], axis_dim, margin)
    return field


def reference(recorded, spectral_weight, psf_taps):
    combined = spectral_weight[0] * jnp.fft.fftn(recorded[0])
    for viewer in range(1, VIEWS):
        combined = combined + spectral_weight[viewer] * jnp.fft.fftn(recorded[viewer])
    joined_volume = jnp.real(jnp.fft.ifftn(combined)).astype(jnp.float32)
    kernels = psf_taps / jnp.sum(psf_taps, axis=-1, keepdims=True)
    margin = TAPS // 2
    estimate = 0.1 + jax.nn.softplus(joined_volume)
    for repeat in range(ITERS):
        summed = jnp.zeros_like(estimate)
        for viewer in range(VIEWS):
            blurred = blur_field(estimate, kernels[viewer], margin)
            ratio = recorded[viewer] / blurred
            summed = summed + blur_field(ratio, kernels[viewer][:, ::-1], margin)
        estimate = estimate * summed / VIEWS
    return joined_volume, estimate
```

```python
import math

import jax
import jax.numpy as jnp
from jax import lax
from jax.experimental import pallas as pl
from jax.experimental.pallas import tpu as pltpu
from jax.sharding import PartitionSpec as P

ITERS = 2


def padded_2(shard, sides, width):
    for axis, dim in sides:
        devices, length = (lax.axis_size(axis), shard.shape[dim])
        before, after = ([], [])
        for hop in range(1, -(-width // length) + 1):
            take = min(length, width - (hop - 1) * length)
            up = [(i, i + hop) for i in range(devices - hop)]
            down = [(j, i) for i, j in up]
            last = lax.slice_in_dim(shard, length - take, length, axis=dim)
            leading = lax.slice_in_dim(shard, 0, take, axis=dim)
            before.insert(0, lax.ppermute(last, axis, up))
            after.append(lax.ppermute(leading, axis, down))
        shard = jnp.concatenate([*before, shard, *after], axis=dim)
    return shard


def tables(length):
    positions = jnp.arange(length, dtype=jnp.int32)
    product = positions[:, None] * positions[None, :] % length
    phases = product.astype(jnp.float32) * (2.0 * math.pi / length)
    return (jnp.cos(phases), jnp.sin(phases))


def mix(form, left, right):
    return jnp.einsum(form, left, right, precision=lax.Precision.HIGH)


def forward_matrix(length):
    c, s = tables(length)
    return jnp.stack([jnp.stack([c, s]), jnp.stack([-s, c])])


def inverse_matrix(length):
    c, s = tables(length)
    return jnp.stack([jnp.stack([c, -s]), jnp.stack([s, c])])


def row_forward(length):
    half = length // 2
    c, s = tables(length)
    imag = jnp.concatenate([c[:, half:half + 1], -s[:, 1:half]], axis=1)
    return jnp.stack([c[:, :half], imag])


def row_inverse(length, total):
    half = length // 2
    c, s = tables(length)
    real = jnp.concatenate([c[:1], 2.0 * c[1:half]], axis=0)
    imag = jnp.concatenate([c[half:half + 1], -2.0 * s[1:half]], axis=0)
    return jnp.stack([real, imag]) / float(total)


def mirrored(block, dim_z, dim_y):
    devices = lax.axis_size("pencil")
    n_z, n_y = (block.shape[dim_z], block.shape[dim_y])
    flipped = lax.rev(block, (dim_z, dim_y))
    flipped = jnp.concatenate(
        [
            lax.slice_in_dim(flipped, n_z - 1, n_z, axis=dim_z),
            lax.slice_in_dim(flipped, 0, n_z - 1, axis=dim_z),
        ],
        axis=dim_z,
    )
    far = lax.ppermute(
        lax.slice_in_dim(flipped, 0, n_y - 1, axis=dim_y),
        "pencil",
        [(i, devices - 1 - i) for i in range(devices)],
    )
    edge = lax.ppermute(
        lax.slice_in_dim(flipped, n_y - 1, n_y, axis=dim_y),
        "pencil",
        [(i, (devices - i) % devices) for i in range(devices)],
    )
    return jnp.concatenate([edge, far], axis=dim_y)


def halves(value):
    high = value.astype(jnp.bfloat16)
    low = (value - high.astype(jnp.float32)).astype(jnp.bfloat16)
    return high, low


def dot3(a, b):
    def one(u, w):
        return lax.dot_general(u, w, (((1,), (0,)), ((), ())), preferred_element_type=jnp.float32)

    return one(a[0], b[0]) + (one(a[0], b[1]) + one(a[1], b[0]))


def band(taps, outs, ins, offset):
    place = jnp.arange(ins)[None, :] - jnp.arange(outs)[:, None] + offset
    result = jnp.zeros((taps.shape[0], outs, ins), jnp.float32)
    for t in range(taps.shape[1]):
        result = result + jnp.where(place == t, 1.0, 0.0)[None] * taps[:, t][:, None, None]
    return result


def rl_step(padded, recorded, taps, mats, out_shape):
    views, depth1, rows1, width = recorded.shape
    depth, rows, _ = out_shape
    n_taps = taps.shape[2]
    margin = n_taps // 2
    rows2 = padded.shape[1]
    chunk = math.gcd(2 * margin, depth)

    def kernel(taps_ref, pad_ref, rec_ref, byh, byl, bxh, bxl, cyh, cyl, cxh, cxl, out_ref, ratio_ref):
        view = pl.program_id(0)

        def z_conv(ref, base, reverse):
            acc = None
            for t in range(n_taps):
                tap = taps_ref[view, 0, n_taps - 1 - t if reverse else t]
                term = tap * ref[pl.ds(base + t, chunk)]
                acc = term if acc is None else acc + term
            return acc

        def planes(value, x_high, x_low, y_high, y_low):
            n, r, w = value.shape
            flat = dot3(halves(value.reshape(n * r, w)), (x_high[0], x_low[0]))
            result = []
            for i in range(n):
                plane = halves(flat[i * r:(i + 1) * r])
                result.append(dot3((y_high[0], y_low[0]), plane))
            return result

        @pl.loop(0, depth1 // chunk)
        def _(c):
            base = c * chunk
            for i, blurred in enumerate(planes(z_conv(pad_ref, base, False), bxh, bxl, byh, byl)):
                ratio_ref[base + i] = rec_ref[0, base + i] / blurred

        @pl.loop(0, depth // chunk)
        def _(c):
            base = c * chunk
            for i, term in enumerate(planes(z_conv(ratio_ref, base, True), cxh, cxl, cyh, cyl)):
                @pl.when(view == 0)
                def _():
                    out_ref[base + i] = term

                @pl.when(view > 0)
                def _():
                    out_ref[base + i] = out_ref[base + i] + term

        @pl.when(view == views - 1)
        def _():
            @pl.loop(0, depth)
            def _(z):
                own = pad_ref[z + 2 * margin, 2 * margin:2 * margin + rows]
                out_ref[z] = own * out_ref[z] / views

    def per_view(array):
        return pl.BlockSpec((1,) + array.shape[1:], lambda v: (v,) + (0,) * (array.ndim - 1))

    return pl.pallas_call(
        kernel,
        grid=(views,),
        in_specs=[
            pl.BlockSpec(memory_space=pltpu.SMEM),
            pl.BlockSpec(padded.shape, lambda v: (0, 0, 0)),
            per_view(recorded),
        ] + [per_view(m) for m in mats],
        out_specs=pl.BlockSpec(out_shape, lambda v: (0, 0, 0)),
        out_shape=jax.ShapeDtypeStruct(out_shape, jnp.float32),
        scratch_shapes=[pltpu.VMEM((depth1, rows1, width), jnp.float32)],
        compiler_params=pltpu.CompilerParams(
            dimension_semantics=("arbitrary",), vmem_limit_bytes=60 * 1024 * 1024
        ),
    )(taps, padded, recorded, *mats)


def body(recorded, spectral_weight, psf_taps):
    views = lax.axis_size("view")
    pencils = lax.axis_size("pencil")
    slab = recorded[0]
    depth, n_y, n_x = slab.shape
    n_z = depth * pencils
    half = n_x // 2
    lines = n_y // pencils
    quarter = n_y // views

    weights = spectral_weight[0]
    columns = jnp.arange(n_x)
    turn = jnp.where(columns[:, None] == (n_x - columns[None, :half]) % n_x, 1.0, 0.0)
    turned = jnp.einsum("kqx,xh->kqh", weights, turn, precision=lax.Precision.HIGHEST)
    sym = 0.5 * (weights[:, :, :half] + mirrored(turned, 0, 1))
    nyquist = weights[:, :, half]
    sym_half = 0.5 * (nyquist + mirrored(nyquist, 0, 1))

    first = mix("zyx,dxh->zdyh", slab, row_forward(n_x))
    second = mix("cdqy,zdyh->qczh", forward_matrix(n_y), first)
    second = second.reshape(pencils, lines, 2, depth, half)
    second = lax.all_to_all(second, "pencil", split_axis=0, concat_axis=0, tiled=True)
    fz = forward_matrix(n_z).reshape(2, 2, n_z, pencils, depth)
    spec = mix("edkpz,pqdzh->qekh", fz, second)

    packed = spec[:, :, :, 0]
    other = mirrored(packed, 2, 0) * jnp.array([1.0, -1.0])[None, :, None]
    w_zero = sym[:, :, 0].T[:, None]
    w_half = sym_half.T[:, None]
    column = 0.5 * (packed * (w_zero + w_half) + other * (w_zero - w_half))
    weighted = spec * jnp.transpose(sym, (1, 0, 2))[:, None]
    lane = jnp.arange(half)
    weighted = jnp.where(lane == 0, column[..., None], weighted)
    summed = lax.psum_scatter(weighted, "view", scatter_dimension=0, tiled=True)

    iz = mix("dezk,qekh->zdqh", inverse_matrix(n_z), summed)
    own_z = n_z // (pencils * views)
    own_q = lines // views
    iz = iz.reshape(pencils * views, own_z, 2, own_q, half)
    iz = lax.all_to_all(iz, ("pencil", "view"), split_axis=0, concat_axis=0, tiled=True)
    my = inverse_matrix(n_y).reshape(2, 2, n_y, pencils * views, own_q)
    iy = mix("edysq,szdqh->zeyh", my, iz)
    thin = mix("zeyh,ehx->zyx", iy, row_inverse(n_x, n_z * n_y * n_x))
    joined_volume = lax.all_to_all(thin, "view", split_axis=1, concat_axis=0, tiled=True)

    kernels = psf_taps / jnp.sum(psf_taps, axis=-1, keepdims=True)
    margin = kernels.shape[-1] // 2
    sides = (("view", 1), ("pencil", 0))
    stacked = lax.all_to_all(recorded, "view", split_axis=2, concat_axis=0, tiled=True)
    stacked = padded_2(stacked, (("view", 2), ("pencil", 1)), margin)
    back = kernels[:, :, ::-1]
    mats = (
        *halves(band(kernels[:, 1], quarter + 2 * margin, quarter + 4 * margin, 0)),
        *halves(jnp.swapaxes(band(kernels[:, 2], n_x, n_x, margin), 1, 2)),
        *halves(band(back[:, 1], quarter, quarter + 2 * margin, 0)),
        *halves(jnp.swapaxes(band(back[:, 2], n_x, n_x, margin), 1, 2)),
    )
    local = 0.1 + jax.nn.softplus(joined_volume)
    for _ in range(ITERS):
        padded = padded_2(local, sides, 2 * margin)
        local = rl_step(padded, stacked, kernels, mats, local.shape)
    return (joined_volume, local)


def solution(mesh):
    return jax.shard_map(
        body,
        mesh=mesh,
        in_specs=(P("view", "pencil", None, None), P("view", None, "pencil", None), P()),
        out_specs=(P("pencil", "view", None), P("pencil", "view", None)),
        check_vma=False,
    )
```
